32 devices in a mesh: fsdp: 8 (over z, core), dp: 4 (over y, x).
Axes of the slice: x: 2, y: 2, z: 4, core: 2. Of those that a mesh axis runs over, the one named last changes fastest.
Arguments:
- embedded: bfloat16 [2, 1024, 32, 768], P(None, ('fsdp', 'dp')), may hold values from -6 to 6
- first_drop: int32 [2, 1024, 32, 768], P(None, ('fsdp', 'dp')), may hold values 0 or 1
- second_drop: int32 [2, 1024, 32, 768], P(None, ('fsdp', 'dp')), may hold values 0 or 1
- sent_lengths: int32 [1024], P(('fsdp', 'dp')), may hold values from 1 to 32, as said below
- out_cotangent: bfloat16 [2, 1024, 32, 768], P(None, ('fsdp', 'dp')), may hold values from -6 to 6
- triple_weight: bfloat16 [768, 2304], P(('fsdp', 'dp')), may hold values from -0.21875 to 0.21875
- query_value_bias: bfloat16 [1536], P(('fsdp', 'dp')), may hold values from -1.5 to 1.5
- mixer_weight: bfloat16 [768, 768], P(('fsdp', 'dp')), may hold values from -0.875 to 0.875
- mixer_bias: bfloat16 [768], P(('fsdp', 'dp')), may hold values from -1.5 to 1.5
- first_gain: bfloat16 [768], P(('fsdp', 'dp')), may hold values from 0.5 to 1.5
- first_shift: bfloat16 [768], P(('fsdp', 'dp')), may hold values from -1.5 to 1.5
- widen_weight: bfloat16 [768, 3072], P(('fsdp', 'dp')), may hold values from -0.21875 to 0.21875
- widen_bias: bfloat16 [3072], P(('fsdp', 'dp')), may hold values from -1.5 to 1.5
- narrow_weight: bfloat16 [3072, 768], P(('fsdp', 'dp')), may hold values from -0.109375 to 0.109375
- narrow_bias: bfloat16 [768], P(('fsdp', 'dp')), may hold values from -1.5 to 1.5
- second_gain: bfloat16 [768], P(('fsdp', 'dp')), may hold values from 0.5 to 1.5
- second_shift: bfloat16 [768], P(('fsdp', 'dp')), may hold values from -1.5 to 1.5
- pooler_weight: bfloat16 [768, 768], P(('fsdp', 'dp')), may hold values from -0.21875 to 0.21875
- pooler_bias: bfloat16 [768], P(('fsdp', 'dp')), may hold values from -1.5 to 1.5
Outputs:
- loss: float32 [], replicated
- outputs: bfloat16 [2, 1024, 32, 768], P(None, ('fsdp', 'dp'))
- input_grad: bfloat16 [2, 1024, 32, 768], P(None, ('fsdp', 'dp'))
- rms_stats: float32 [3], replicated
- grad_triple_weight: float32 [768, 2304], P(('fsdp', 'dp'))
- grad_query_value_bias: float32 [1536], P(('fsdp', 'dp'))
- grad_mixer_weight: float32 [768, 768], P(('fsdp', 'dp'))
- grad_mixer_bias: float32 [768], P(('fsdp', 'dp'))
- grad_first_gain: float32 [768], P(('fsdp', 'dp'))
- grad_first_shift: float32 [768], P(('fsdp', 'dp'))
- grad_widen_weight: float32 [768, 3072], P(('fsdp', 'dp'))
- grad_widen_bias: float32 [3072], P(('fsdp', 'dp'))
- grad_narrow_weight: float32 [3072, 768], P(('fsdp', 'dp'))
- grad_narrow_bias: float32 [768], P(('fsdp', 'dp'))
- grad_second_gain: float32 [768], P(('fsdp', 'dp'))
- grad_second_shift: float32 [768], P(('fsdp', 'dp'))
- grad_pooler_weight: float32 [768, 768], P(('fsdp', 'dp'))
- grad_pooler_bias: float32 [768], P(('fsdp', 'dp'))
The draws below stay inside these ranges and needn't reach their ends.
Inputs may be any that keep to these rules, and one draw needn't show every extreme that they name: `sent_lengths`: the sentences of one device lie in a bucket of lengths b - 32 // 4 + 1 to b, where b lies between 8 and 32 ; the first sentence of each device has length b, and some device has b = 32.
All inputs are finite; a program needn't handle non-finite values. No bound on the sum of `first_drop` or of `second_drop` on one device may be relied on, other than what follows from the above.
Results may differ from the reference program's by a relative error of at most 0.014.
Values may be sent and summed in bfloat16 or wider, within the bound.
No kernel may reach another device: no remote copies, remote signals or barrier semaphores. Data moves between devices by JAX's collectives and lax.ppermute only.
A program may use at most 384 MiB of HBM per device.

```python
import math
import jax
import jax.numpy as jnp
from jax import lax

D = 768
HEADS = 12
HEAD_SIZE = 64
FF = 3072
PAD_LEN = 32
SENT_DEV = 32
SENTS = 1024


def draw_embedded(key, part):
    shared_key, own_key = jax.random.split(key)
    shared = jax.random.normal(shared_key, (1, SENTS, PAD_LEN, D), jnp.float32)
    own_part = jax.random.normal(own_key, (2, SENTS, PAD_LEN, D), jnp.float32)
    return jnp.clip(0.8 * shared + 0.6 * own_part, -6.0, 6.0).astype(jnp.bfloat16)


def draw_sent_lengths(key, part):
    device_total = SENTS // SENT_DEV
    order_key, length_key = jax.random.split(key)
    bucket_rank = jax.random.permutation(order_key, device_total).astype(jnp.int32)
    least_top = PAD_LEN // 4
    bucket_top = least_top + (PAD_LEN - least_top) * bucket_rank // max(device_total - 1, 1)
    bucket_low = jnp.maximum(bucket_top - least_top + 1, 1)
    drawn = jax.random.randint(length_key, (device_total, SENT_DEV), bucket_low[:, None], bucket_top[:, None] + 1)
    drawn = drawn.at[:, 0].set(bucket_top)
    return drawn.reshape(SENTS).astype(jnp.int32)


def touch_ends(values, key, least, high):
    extent = values.shape
    spot = [jax.random.randint(jax.random.fold_in(key, axis), (), 0, extent[axis]) for axis in range(len(extent))]
    values = values.at[tuple(spot)].set(least)
    longest = extent.index(max(extent))
    spot[longest] = (spot[longest] + 1) % extent[longest]
    return values.at[tuple(spot)].set(high)


def levels(key, shape, shards, low, top_value):
    def one(position, parts):
        heights = jax.random.uniform(jax.random.fold_in(jax.random.fold_in(key, 6), position), (parts,), jnp.float32, low / len(shards), top_value / len(shards))
        return jnp.repeat(jnp.exp(heights), shape[position] // parts).reshape((-1,) + (1,) * (len(shape) - position - 1))

    loudness = one(*shards[0])
    for cut in shards[1:]:
        loudness = loudness * one(*cut)
    return loudness


def noise(key, extent, scale, most, pieces=(), kind=jnp.bfloat16):
    result = scale * jax.random.normal(key, extent, jnp.float32)
    if pieces:
        result = result * levels(key, extent, pieces, -0.22, 0.18)
    return jnp.clip(result, -most, most).astype(kind)


def setup_inputs(seed: int = 0) -> dict:
    streams_of = jax.random.split(jax.random.key(seed), 20)
    embedded = draw_embedded(jax.random.fold_in(streams_of[19], 71), 0)
    first_drop = touch_ends((jax.random.randint(streams_of[1], (2, SENTS, PAD_LEN, D), 0, 10) < 9).astype(jnp.int32), jax.random.fold_in(streams_of[1], 1), 0, 1)
    second_drop = touch_ends((jax.random.randint(streams_of[2], (2, SENTS, PAD_LEN, D), 0, 10) < 9).astype(jnp.int32), jax.random.fold_in(streams_of[2], 1), 0, 1)
    sent_lengths = draw_sent_lengths(jax.random.fold_in(streams_of[19], 71), 0)
    out_cotangent = noise(streams_of[4], (2, SENTS, PAD_LEN, D), 1.0, 6.0, ((1, 32),))
    triple_weight = noise(streams_of[5], (D, 3 * D), D ** -0.5, 0.21875, ((0, 32),))
    query_value_bias = noise(streams_of[6], (2 * D,), 0.3, 1.5, ((0, 32),))
    mixer_weight = noise(streams_of[7], (D, D), (D // 16) ** -0.5, 0.875, ((0, 32),))
    mixer_bias = noise(streams_of[8], (D,), 0.3, 1.5, ((0, 32),))
    first_gain = jnp.clip(1.0 + 0.1 * jax.random.normal(streams_of[9], (D,), jnp.float32), 0.5, 1.5).astype(jnp.bfloat16)
    first_shift = noise(streams_of[10], (D,), 0.3, 1.5, ((0, 32),))
    widen_weight = noise(streams_of[11], (D, FF), D ** -0.5, 0.21875, ((0, 32),))
    widen_bias = noise(streams_of[12], (FF,), 0.3, 1.5, ((0, 32),))
    narrow_weight = noise(streams_of[13], (FF, D), FF ** -0.5, 0.109375, ((0, 32),))
    narrow_bias = noise(streams_of[14], (D,), 0.3, 1.5, ((0, 32),))
    second_gain = jnp.clip(1.0 + 0.1 * jax.random.normal(streams_of[15], (D,), jnp.float32), 0.5, 1.5).astype(jnp.bfloat16)
    second_shift = noise(streams_of[16], (D,), 0.3, 1.5, ((0, 32),))
    pooler_weight = noise(streams_of[17], (D, D), D ** -0.5, 0.21875, ((0, 32),))
    pooler_bias = noise(streams_of[18], (D,), 0.3, 1.5, ((0, 32),))
    return dict(embedded=embedded, first_drop=first_drop, second_drop=second_drop, sent_lengths=sent_lengths, out_cotangent=out_cotangent, triple_weight=triple_weight, query_value_bias=query_value_bias, mixer_weight=mixer_weight, mixer_bias=mixer_bias, first_gain=first_gain, first_shift=first_shift, widen_weight=widen_weight, widen_bias=widen_bias, narrow_weight=narrow_weight, narrow_bias=narrow_bias, second_gain=second_gain, second_shift=second_shift, pooler_weight=pooler_weight, pooler_bias=pooler_bias)


DROP_SCALE = 1.0 / 0.9
SOFTMAX_TEMP = 0.05

@jax.custom_vjp
def low(v):
    return lax.optimization_barrier(v.astype(jnp.bfloat16)).astype(jnp.float32)

@jax.custom_vjp
def low_back(v):
    return v

def low_keep(v):
    return (low(v), None)

def low_pass(kept, grad):
    return (grad,)

def back_keep(v):
    return (v, None)

def back_low(kept, grad):
    return (low(grad),)
low.defvjp(low_keep, low_pass)
low_back.defvjp(back_keep, back_low)

def product(left_side, right_side):
    return jnp.dot(left_side, right_side, precision=lax.Precision.HIGHEST, preferred_element_type=jnp.float32)

def layer_norm(values, norm_gain, norm_shift):
    centred = values - lax.optimization_barrier(jnp.mean(values, axis=-1, keepdims=True))
    spread = lax.optimization_barrier(jnp.mean(centred * centred, axis=-1, keepdims=True))
    return centred * lax.rsqrt(spread + 1e-12) * norm_gain + norm_shift

def pool_unit(pooler_input):
    pooled = jnp.tanh(pooler_input)
    return pooled * lax.rsqrt(lax.optimization_barrier(jnp.sum(pooled * pooled, axis=-1, keepdims=True)) + 1e-06)

def group_layer(layer_weights, inputs, drop_one, drop_two, lengths):
    triple, query_value, mixer, mixer_shift, gain_one, shift_one, widen, widen_shift, narrow, narrow_shift, gain_two, shift_two = layer_weights
    view_count, group_size, length, model_width = inputs.shape
    valid_bool = jnp.arange(length, dtype=jnp.int32)[None, :] < lengths[:, None]
    valid_mask = valid_bool.astype(jnp.float32)
    valid_rows = jnp.broadcast_to(valid_mask[None], (view_count, group_size, length)).reshape(-1, 1)
    valid_keys = jnp.tile(valid_bool, (view_count, 1))
    row_data = inputs.reshape(-1, model_width)
    bias_full = jnp.concatenate([query_value[:model_width], jnp.zeros((model_width,), jnp.float32), query_value[model_width:]])
    packed = low_back(low(product(row_data, triple) + bias_full))
    packed = packed.reshape(view_count * group_size, length, 3, HEADS, HEAD_SIZE)
    queries = packed[:, :, 0]
    key_rows = packed[:, :, 1]
    values = packed[:, :, 2]
    scores = jnp.einsum('sqhe,skhe->shqk', queries, key_rows, precision=lax.Precision.HIGHEST) * HEAD_SIZE ** (-0.5)
    scores = low_back(jnp.where(valid_keys[:, None, None, :], scores, -1000000000.0))
    attention_low = low(jax.nn.softmax(scores, axis=-1))
    context = jnp.einsum('shqk,skhe->sqhe', attention_low, values, precision=lax.Precision.HIGHEST).reshape(-1, model_width)
    context = low_back(low(context))
    branch = low_back(product(context, mixer) + mixer_shift)
    attn_part = branch * drop_one.reshape(-1, model_width)
    residual = row_data + attn_part
    hidden = layer_norm(residual, gain_one, shift_one)
    widened = low_back(product(low(hidden), widen) + widen_shift)
    active = low(jax.nn.gelu(widened, approximate=False))
    narrowed = low_back(product(active, narrow) + narrow_shift)
    ffn_part = narrowed * drop_two.reshape(-1, model_width)
    second = hidden + ffn_part
    normed = layer_norm(second, gain_two, shift_two) * valid_rows
    first_token = low(normed.reshape(view_count, group_size, length, model_width)[:, :, 0])
    sums = jnp.stack([jnp.sum(valid_rows * row_data * row_data), jnp.sum(valid_rows * attn_part * attn_part), jnp.sum(valid_rows * ffn_part * ffn_part)])
    return (normed.reshape(inputs.shape), first_token, sums)

def pair_loss(first_token, pool_weight, pool_shift):
    pooler_input = low_back(product(first_token, pool_weight) + pool_shift)
    unit_rows = low(pool_unit(pooler_input)).reshape(2, SENTS, D)
    first_unit = unit_rows[0]
    second_unit = unit_rows[1]
    block_rows = math.gcd(SENTS, 256)

    def block_loss(block_item):
        rows_block, first_row = block_item
        cosine_similarity = low_back(product(rows_block, second_unit.T))
        scaled_logits = cosine_similarity / SOFTMAX_TEMP
        log_total = jax.nn.logsumexp(scaled_logits, axis=-1)
        local_part = lax.dynamic_slice_in_dim(scaled_logits, first_row, block_rows, 1)
        return log_total - jnp.diagonal(local_part)
    starts = jnp.arange(SENTS // block_rows, dtype=jnp.int32) * block_rows
    per_row = lax.map(jax.checkpoint(block_loss), (first_unit.reshape(-1, block_rows, D), starts))
    return jnp.sum(per_row) / SENTS

def reference(embedded, first_drop, second_drop, sent_lengths, out_cotangent, triple_weight, query_value_bias, mixer_weight, mixer_bias, first_gain, first_shift, widen_weight, widen_bias, narrow_weight, narrow_bias, second_gain, second_shift, pooler_weight, pooler_bias):
    weight_list = tuple((item.astype(jnp.float32) for item in (triple_weight, query_value_bias, mixer_weight, mixer_bias, first_gain, first_shift, widen_weight, widen_bias, narrow_weight, narrow_bias, second_gain, second_shift, pooler_weight, pooler_bias)))
    inputs = embedded.astype(jnp.float32)
    drop_one = first_drop.astype(jnp.float32) * DROP_SCALE
    drop_two = second_drop.astype(jnp.float32) * DROP_SCALE
    group_size = math.gcd(SENTS, 64)
    group_total = SENTS // group_size

    def regroup(array):
        return jnp.moveaxis(array.reshape((2, group_total, group_size) + array.shape[2:]), 1, 0)

    def objective(weight_set, layer_input):
        layer_weights = weight_set[:12]

        def one_group(carry_in, group_item):
            normed, first_token, sums = group_layer(layer_weights, *group_item)
            return (carry_in, (normed, first_token, sums))
        scan_items = (regroup(layer_input), regroup(drop_one), regroup(drop_two), sent_lengths.reshape(group_total, group_size))
        carry_out, (normed, first_token, sums) = lax.scan(jax.checkpoint(one_group), jnp.zeros((), jnp.float32), scan_items)
        normed = jnp.moveaxis(normed, 0, 1).reshape(2, SENTS, PAD_LEN, D)
        first_token = jnp.moveaxis(first_token, 0, 1).reshape(2 * SENTS, D)
        loss_value = pair_loss(first_token, weight_set[12], weight_set[13])
        return ((loss_value, normed), lax.optimization_barrier(jnp.sum(sums, axis=0)))
    (loss_value, normed), back_fn, sums = jax.vjp(objective, weight_list, inputs, has_aux=True)
    loss_seed = jnp.full((), SENTS, jnp.float32)
    weight_grads, input_grad = back_fn((loss_seed, out_cotangent.astype(jnp.float32)))
    token_count = 2.0 * jnp.sum(sent_lengths).astype(jnp.float32) * D
    rms_stats = jnp.sqrt(sums / token_count)
    return (loss_value, normed.astype(jnp.bfloat16), input_grad.astype(jnp.bfloat16), rms_stats, weight_grads[0], weight_grads[1], weight_grads[2], weight_grads[3], weight_grads[4], weight_grads[5], weight_grads[6], weight_grads[7], weight_grads[8], weight_grads[9], weight_grads[10], weight_grads[11], weight_grads[12], weight_grads[13])
```

```python
import functools

import jax
import jax.numpy as jnp
from jax import lax
from jax.experimental import pallas as pl
from jax.experimental.pallas import tpu as pltpu
from jax.sharding import PartitionSpec as P

HEADS = 12
DROP_SCALE = 1.0 / 0.9
SOFTMAX_TEMP = 0.05
INV_TEMP = 20.0
AXES = ("fsdp", "dp")
F32 = jnp.float32
BF16 = jnp.bfloat16
LANES = 128
MASKED = -1e30
ROWS = 256
SUB = 128
VMEM_LIMIT = 60 * 1024 * 1024
ROOT_HALF = 0.7071067811865476
INV_ROOT_TAU = 0.3989422804014327


def dot(a, b):
    return jnp.dot(a, b, preferred_element_type=F32)


def dot_nt(a, b):
    return lax.dot_general(a, b, (((1,), (1,)), ((), ())), preferred_element_type=F32)


def dot_tn(a, b):
    return lax.dot_general(a, b, (((0,), (0,)), ((), ())), preferred_element_type=F32)


def iota(shape, dim):
    return lax.broadcasted_iota(jnp.int32, shape, dim)


def head_masks():
    lane = iota((1, LANES), 1)
    return lane < 64, lane >= 64


def two_heads(rows, scale):
    low, high = head_masks()
    s = jnp.asarray(scale, BF16)
    zero = jnp.zeros_like(rows)
    scaled = rows * s if scale != 1.0 else rows
    return jnp.concatenate([jnp.where(low, scaled, zero), jnp.where(high, scaled, zero)], axis=0)


def lane_lengths(lens_ref, first, count, group, shape, dim):
    where = iota(shape, dim) // group
    out = jnp.zeros(shape, jnp.int32)
    for k in range(count):
        out = jnp.where(where == k, lens_ref[first + k], out)
    return out


def row_valid(lens_ref, step, rows, length):
    per = rows // length
    first = lax.rem(step * per, lens_ref.shape[0])
    shape = (rows, LANES)
    lens = lane_lengths(lens_ref, first, per, length, shape, 0)
    return (iota(shape, 0) % length < lens).astype(F32)


def masked_square(values, valid):
    total = None
    for c in range(values.shape[1] // LANES):
        part = values[:, c * LANES : (c + 1) * LANES]
        part = part * part * valid
        total = part if total is None else total + part
    return jnp.sum(total.reshape(-1, 8, LANES), axis=0)


def normalise(values):
    centred = values - jnp.mean(values, axis=-1, keepdims=True)
    rho = lax.rsqrt(jnp.mean(centred * centred, axis=-1, keepdims=True) + 1e-12)
    return centred * rho, rho


def norm_back(dout, c, rho, gain):
    dg = dout * gain
    return rho * (
        dg - jnp.mean(dg, axis=-1, keepdims=True) - c * jnp.mean(dg * c, axis=-1, keepdims=True)
    )


def attn_fwd_kernel(
    lens_ref, x_ref, drop_ref, w_ref, wb_ref, m_ref, mb_ref,
    packed_ref, p_ref, ctx_ref, c_ref, rho_ref, first_ref, sums_ref,
    *, length,
):
    step = pl.program_id(0)
    x = x_ref[...]
    width = x.shape[1]
    for t in range(3):
        cols = slice(t * width, (t + 1) * width)
        packed_ref[:, cols] = (dot(x, w_ref[:, cols]) + wb_ref[:, cols]).astype(BF16)
    per = SUB // length
    for u in range(ROWS // SUB):
        rows = slice(u * SUB, (u + 1) * SUB)
        first = lax.rem(step * (ROWS // length) + u * per, lens_ref.shape[0])
        shape = (SUB, SUB)
        lens = lane_lengths(lens_ref, first, per, length, shape, 1)
        lane = iota(shape, 1)
        seen = (iota(shape, 0) // length == lane // length) & (lane % length < lens)
        bias = jnp.where(seen, 0.0, MASKED).astype(F32)
        for pair in range(width // LANES):
            a = pair * LANES
            q = packed_ref[rows, a : a + LANES]
            k = packed_ref[rows, width + a : width + a + LANES]
            v = packed_ref[rows, 2 * width + a : 2 * width + a + LANES]
            scores = dot_nt(q, two_heads(k, 0.125))
            halves = []
            for h in range(2):
                s = scores[:, h * SUB : (h + 1) * SUB] + bias
                e = jnp.exp(s - jnp.max(s, axis=-1, keepdims=True))
                halves.append((e * (1.0 / jnp.sum(e, axis=-1, keepdims=True))).astype(BF16))
            p = jnp.concatenate(halves, axis=1)
            p_ref[rows, pair * 2 * SUB : (pair + 1) * 2 * SUB] = p
            ctx_ref[rows, a : a + LANES] = dot(p, two_heads(v, 1.0)).astype(BF16)
    branch = dot(ctx_ref[...], m_ref[...]) + mb_ref[...]
    part = branch * (drop_ref[...].astype(F32) * DROP_SCALE)
    xf = x.astype(F32)
    valid = row_valid(lens_ref, step, ROWS, length)
    sums_ref[0, 0] = masked_square(xf, valid)
    sums_ref[0, 1] = masked_square(part, valid)
    c, rho = normalise(xf + part)
    c_ref[...] = c
    rho_ref[...] = rho
    first_ref[...] = jnp.concatenate(
        [c[k * length : k * length + 1] for k in range(ROWS // length)], axis=0
    )


def resident(shape, column=0):
    return pl.BlockSpec(shape, lambda *_: (0, column), pipeline_mode=pl.Buffered(1))


MIXER, POOLER = 4, 5


def row_block(cols, rows=ROWS):
    return pl.BlockSpec((rows, cols), lambda i, *_: (i, 0))


def params():
    return pltpu.CompilerParams(vmem_limit_bytes=VMEM_LIMIT)


def attn_fwd(lens, x, drop, weights, wb, mixer, mb, length):
    n, d = x.shape
    steps = n // ROWS
    per = ROWS // length
    f = lambda cols, t, rows=n: jax.ShapeDtypeStruct((rows, cols), t)
    return pl.pallas_call(
        functools.partial(attn_fwd_kernel, length=length),
        name="attn_fwd",
        grid_spec=pltpu.PrefetchScalarGridSpec(
            num_scalar_prefetch=1,
            grid=(steps,),
            in_specs=[
                row_block(d), row_block(d),
                resident((d, 3 * d)), resident((1, 3 * d)), resident((d, d), MIXER), resident((1, d)),
            ],
            out_specs=[
                row_block(3 * d), row_block(2 * d), row_block(d), row_block(d), row_block(1),
                row_block(d, per), pl.BlockSpec((1, 2, 8, LANES), lambda i, *_: (i, 0, 0, 0)),
            ],
        ),
        out_shape=[
            f(3 * d, BF16), f(2 * d, BF16), f(d, BF16), f(d, F32), f(1, F32),
            f(d, F32, steps * per), jax.ShapeDtypeStruct((steps, 2, 8, LANES), F32),
        ],
        compiler_params=params(),
        cost_estimate=pl.CostEstimate(
            flops=2 * n * d * d * 6, bytes_accessed=n * d * 26, transcendentals=n * d
        ),
    )(lens, x, drop, weights, wb, mixer, mb)


CHUNK = 512


def ffn_chunk(hl, ww_ref, wwb_ref, cols):
    u = dot(hl, ww_ref[:, cols]) + wwb_ref[:, cols]
    phi = 0.5 + 0.5 * lax.erf(u * ROOT_HALF)
    return u, phi


def ffn_fwd_kernel(
    lens_ref, c_ref, drop_ref, g1_ref, s1_ref, ww_ref, wwb_ref, wn_ref, wnb_ref, g2_ref, s2_ref,
    hl_ref, act_ref, slope_ref, c2_ref, rho_ref, out_ref, sums_ref,
    *, length,
):
    step = pl.program_id(0)
    hidden = c_ref[...] * g1_ref[...] + s1_ref[...]
    hl = hidden.astype(BF16)
    hl_ref[...] = hl
    total = None
    for ch in range(ww_ref.shape[1] // CHUNK):
        cols = slice(ch * CHUNK, (ch + 1) * CHUNK)
        u, phi = ffn_chunk(hl, ww_ref, wwb_ref, cols)
        act = (u * phi).astype(BF16)
        act_ref[:, cols] = act
        slope_ref[:, cols] = (phi + u * (jnp.exp(u * u * -0.5) * INV_ROOT_TAU)).astype(BF16)
        part = dot(act, wn_ref[cols, :])
        total = part if total is None else total + part
    part = (total + wnb_ref[...]) * (drop_ref[...].astype(F32) * DROP_SCALE)
    valid = row_valid(lens_ref, step, ROWS, length)
    sums_ref[0] = masked_square(part, valid)
    c2, rho = normalise(hidden + part)
    c2_ref[...] = c2
    rho_ref[...] = rho
    normed = c2 * g2_ref[...] + s2_ref[...]
    out_ref[...] = (normed * valid[:, :1]).astype(BF16)


def ffn_fwd(lens, c, drop, g1, s1, ww, wwb, wn, wnb, g2, s2, length):
    n, d = c.shape
    ff = wn.shape[0]
    steps = n // ROWS
    f = lambda cols, t, rows=n: jax.ShapeDtypeStruct((rows, cols), t)
    return pl.pallas_call(
        functools.partial(ffn_fwd_kernel, length=length),
        name="ffn_fwd",
        grid_spec=pltpu.PrefetchScalarGridSpec(
            num_scalar_prefetch=1,
            grid=(steps,),
            in_specs=[
                row_block(d), row_block(d), resident((1, d)), resident((1, d)),
                resident((d, ff)), resident((1, ff)), resident((ff, d)), resident((1, d)),
                resident((1, d)), resident((1, d)),
            ],
            out_specs=[
                row_block(d), row_block(ff), row_block(ff), row_block(d), row_block(1),
                row_block(d), pl.BlockSpec((1, 8, LANES), lambda i, *_: (i, 0, 0)),
            ],
        ),
        out_shape=[
            f(d, BF16), f(ff, BF16), f(ff, BF16), f(d, F32), f(1, F32), f(d, BF16),
            jax.ShapeDtypeStruct((steps, 8, LANES), F32),
        ],
        compiler_params=params(),
        cost_estimate=pl.CostEstimate(
            flops=4 * n * d * ff, bytes_accessed=n * d * 32, transcendentals=2 * n * ff
        ),
    )(lens, c, drop, g1, s1, ww, wwb, wn, wnb, g2, s2)


def first_kernel(
    c_ref, drop_ref, g1_ref, s1_ref, ww_ref, wwb_ref, wn_ref, wnb_ref, g2_ref, s2_ref,
    wp_ref, wpb_ref, unit_ref, pooled_ref, rho_ref, first_ref,
):
    hidden = c_ref[...] * g1_ref[...] + s1_ref[...]
    hl = hidden.astype(BF16)
    total = None
    for ch in range(ww_ref.shape[1] // CHUNK):
        cols = slice(ch * CHUNK, (ch + 1) * CHUNK)
        u, phi = ffn_chunk(hl, ww_ref, wwb_ref, cols)
        part = dot((u * phi).astype(BF16), wn_ref[cols, :])
        total = part if total is None else total + part
    part = (total + wnb_ref[...]) * (drop_ref[...].astype(F32) * DROP_SCALE)
    c2, _ = normalise(hidden + part)
    first = (c2 * g2_ref[...] + s2_ref[...]).astype(BF16)
    first_ref[...] = first
    pooled = jnp.tanh(dot(first, wp_ref[...]) + wpb_ref[...])
    rho = lax.rsqrt(jnp.sum(pooled * pooled, axis=-1, keepdims=True) + 1e-6)
    pooled_ref[...] = pooled
    rho_ref[...] = rho
    unit_ref[...] = (pooled * rho).astype(BF16)


def first_tokens(c, drop, g1, s1, ww, wwb, wn, wnb, g2, s2, wpb):
    n, d = c.shape
    ff = wn.shape[0]
    vector = resident((1, d))
    f = lambda cols, t: jax.ShapeDtypeStruct((n, cols), t)
    return pl.pallas_call(
        first_kernel,
        name="first_tokens",
        grid=(1,),
        in_specs=[
            resident((n, d)), resident((n, d)), vector, vector, resident((d, ff)), resident((1, ff)),
            resident((ff, d)), vector, vector, vector, resident((d, d), POOLER), vector,
        ],
        out_specs=[resident((n, d)), resident((n, d)), resident((n, 1)), resident((n, d))],
        out_shape=[f(d, BF16), f(d, F32), f(1, F32), f(d, BF16)],
        compiler_params=params(),
    )(c, drop, g1, s1, ww, wwb, wn, wnb, g2, s2, ww, wpb)


def loss_kernel(
    place_ref, one_ref, two_ref, pooled_ref, rho_ref, first_ref, wp_ref,
    loss_ref, dfirst_ref, gw_ref, gb_ref,
):
    total = one_ref.shape[0]
    mine = pooled_ref.shape[0] // 2
    start = pl.multiple_of(place_ref[0] * mine, mine)
    block = 256
    logs, worth = [], jnp.zeros((1, 1), F32)
    for b in range(total // block):
        rows = one_ref[b * block : (b + 1) * block, :]
        similar = dot_nt(two_ref[...], rows)
        log_total = jnp.log(jnp.sum(jnp.exp(similar * INV_TEMP), axis=0, keepdims=True))
        same = iota(similar.shape, 0) == iota(similar.shape, 1) + b * block
        positive = jnp.sum(jnp.where(same, similar, 0.0), axis=0, keepdims=True)
        logs.append(log_total)
        worth = worth + jnp.sum(log_total - positive * INV_TEMP, axis=1, keepdims=True)
    loss_ref[...] = worth * (1.0 / total)
    log_total = jnp.concatenate(logs, axis=1)
    shape = (mine, total)
    same = (iota(shape, 0) + start == iota(shape, 1)).astype(F32)
    similar = dot_nt(two_ref[pl.ds(start, mine), :], one_ref[...])
    dsim = ((jnp.exp(similar * INV_TEMP - log_total) - same) * INV_TEMP).astype(BF16)
    dtwo = dot(dsim, one_ref[...])
    similar = dot_nt(one_ref[pl.ds(start, mine), :], two_ref[...]) * INV_TEMP
    own = jnp.log(jnp.sum(jnp.exp(similar), axis=1, keepdims=True))
    dsim = ((jnp.exp(similar - own) - same) * INV_TEMP).astype(BF16)
    done = dot(dsim, two_ref[...])
    dunit = jnp.concatenate([done, dtwo], axis=0)
    pooled, rho = pooled_ref[...], rho_ref[...]
    inner = jnp.sum(pooled * dunit, axis=-1, keepdims=True)
    dpool = ((1.0 - pooled * pooled) * (rho * dunit - rho * rho * rho * pooled * inner)).astype(BF16)
    dfirst_ref[...] = dot_nt(dpool, wp_ref[...])
    gw_ref[...] = dot_tn(first_ref[...], dpool)
    gb_ref[...] = jnp.sum(dpool.astype(F32), axis=0, keepdims=True)


def loss_parts(place, one, two, pooled, rho, first, wp):
    n, d = pooled.shape
    f = lambda r, c: jax.ShapeDtypeStruct((r, c), F32)
    whole = [one, two, pooled, rho, first]
    return pl.pallas_call(
        loss_kernel,
        name="loss",
        grid=(1,),
        in_specs=[pl.BlockSpec(memory_space=pltpu.SMEM)]
        + [resident(v.shape) for v in whole]
        + [resident((d, d), POOLER)],
        out_specs=[resident((1, 1)), resident((n, d)), resident((d, d)), resident((1, d))],
        out_shape=[f(1, 1), f(n, d), f(d, d), f(1, d)],
        compiler_params=params(),
    )(place, one, two, pooled, rho, first, wp)


def ffn_back_kernel(
    lens_ref, cot_ref, dfirst_ref, c2_ref, rho2_ref, drop2_ref, slope_ref, c_ref, rho_ref, drop_ref,
    g1_ref, ww_ref, wn_ref, g2_ref,
    dnarrow_ref, dwide_ref, dres_ref, dbranch_ref, rows_ref, wide_ref,
    *, length,
):
    step = pl.program_id(0)
    d = c_ref.shape[1]

    @pl.when(step == 0)
    def _():
        rows_ref[...] = jnp.zeros_like(rows_ref)
        wide_ref[...] = jnp.zeros_like(wide_ref)

    def add_row(k, values):
        rows_ref[k : k + 1, :] += jnp.sum(values, axis=0, keepdims=True)

    valid = row_valid(lens_ref, step, ROWS, length)[:, :1]
    per = ROWS // length
    dout = cot_ref[...].astype(F32).reshape(per, length, d)
    is_first = iota((per, length, d), 1) == 0
    dout = dout + jnp.where(is_first, dfirst_ref[...][:, None, :], 0.0)
    dout = dout.reshape(ROWS, d) * valid
    c2 = c2_ref[...]
    add_row(0, dout * c2)
    add_row(1, dout)
    dsecond = norm_back(dout, c2, rho2_ref[...], g2_ref[...])
    dnarrow = (dsecond * (drop2_ref[...].astype(F32) * DROP_SCALE)).astype(BF16)
    dnarrow_ref[...] = dnarrow
    add_row(2, dnarrow.astype(F32))
    dhidden = dsecond
    for ch in range(ww_ref.shape[1] // CHUNK):
        cols = slice(ch * CHUNK, (ch + 1) * CHUNK)
        dactive = dot_nt(dnarrow, wn_ref[cols, :])
        dwide = (dactive * slope_ref[:, cols].astype(F32)).astype(BF16)
        dwide_ref[:, cols] = dwide
        wide_ref[0:1, cols] += jnp.sum(dwide.astype(F32), axis=0, keepdims=True)
        dhidden = dhidden + dot_nt(dwide, ww_ref[:, cols])
    c = c_ref[...]
    add_row(3, dhidden * c)
    add_row(4, dhidden)
    dres = norm_back(dhidden, c, rho_ref[...], g1_ref[...])
    dres_ref[...] = dres
    dbranch = (dres * (drop_ref[...].astype(F32) * DROP_SCALE)).astype(BF16)
    dbranch_ref[...] = dbranch
    add_row(5, dbranch.astype(F32))


def ffn_back(lens, cot, dfirst, c2, rho2, drop2, slope, c, rho, drop, g1, ww, wn, g2, length):
    n, d = c.shape
    ff = wn.shape[0]
    steps = n // ROWS
    f = lambda cols, t, rows=n: jax.ShapeDtypeStruct((rows, cols), t)
    whole = lambda r, c: pl.BlockSpec((r, c), lambda i, *_: (0, 0))
    return pl.pallas_call(
        functools.partial(ffn_back_kernel, length=length),
        name="ffn_back",
        grid_spec=pltpu.PrefetchScalarGridSpec(
            num_scalar_prefetch=1,
            grid=(steps,),
            in_specs=[
                row_block(d), row_block(d, ROWS // length), row_block(d), row_block(1),
                row_block(d), row_block(ff), row_block(d), row_block(1), row_block(d),
                resident((1, d)), resident((d, ff)), resident((ff, d)), resident((1, d)),
            ],
            out_specs=[
                row_block(d), row_block(ff), row_block(d), row_block(d), whole(8, d), whole(8, ff),
            ],
        ),
        out_shape=[f(d, BF16), f(ff, BF16), f(d, F32), f(d, BF16), f(d, F32, 8), f(ff, F32, 8)],
        compiler_params=params(),
        cost_estimate=pl.CostEstimate(
            flops=4 * n * d * ff, bytes_accessed=n * d * 40, transcendentals=0
        ),
    )(lens, cot, dfirst, c2, rho2, drop2, slope, c, rho, drop, g1, ww, wn, g2)


def attn_back_kernel(
    dbranch_ref, dres_ref, packed_ref, p_ref, w_ref, m_ref, dpacked_ref, dx_ref, rows_ref
):
    step = pl.program_id(0)
    width = dres_ref.shape[1]

    @pl.when(step == 0)
    def _():
        rows_ref[...] = jnp.zeros_like(rows_ref)

    low, _ = head_masks()
    dctx = dot_nt(dbranch_ref[...], m_ref[...]).astype(BF16)
    for u in range(ROWS // SUB):
        rows = slice(u * SUB, (u + 1) * SUB)
        for pair in range(width // LANES):
            a = pair * LANES
            q = packed_ref[rows, a : a + LANES]
            k2 = two_heads(packed_ref[rows, width + a : width + a + LANES], 0.125)
            v2 = two_heads(packed_ref[rows, 2 * width + a : 2 * width + a + LANES], 1.0)
            p = p_ref[rows, pair * 2 * SUB : (pair + 1) * 2 * SUB]
            dc = dctx[rows, a : a + LANES]
            dp = dot_nt(dc, v2)
            pf = p.astype(F32)
            parts = []
            for h in range(2):
                cols = slice(h * SUB, (h + 1) * SUB)
                t = pf[:, cols] * dp[:, cols]
                parts.append((t - pf[:, cols] * jnp.sum(t, axis=-1, keepdims=True)).astype(BF16))
            ds = jnp.concatenate(parts, axis=1)
            dpacked_ref[rows, a : a + LANES] = dot(ds, k2).astype(BF16)
            dk = dot_tn(ds, q)
            dk = jnp.where(low, dk[:SUB], dk[SUB:]) * 0.125
            dpacked_ref[rows, width + a : width + a + LANES] = dk.astype(BF16)
            dv = dot_tn(p, dc)
            dv = jnp.where(low, dv[:SUB], dv[SUB:])
            dpacked_ref[rows, 2 * width + a : 2 * width + a + LANES] = dv.astype(BF16)
    total = dres_ref[...]
    for t in range(3):
        cols = slice(t * width, (t + 1) * width)
        part = dpacked_ref[:, cols]
        rows_ref[0:1, cols] += jnp.sum(part.astype(F32), axis=0, keepdims=True)
        total = total + dot_nt(part, w_ref[:, cols])
    dx_ref[...] = total.astype(BF16)


def attn_back(dbranch, dres, packed, p, weights, mixer):
    n, d = dres.shape
    f = lambda cols, t, rows=n: jax.ShapeDtypeStruct((rows, cols), t)
    return pl.pallas_call(
        attn_back_kernel,
        name="attn_back",
        grid=(n // ROWS,),
        in_specs=[
            row_block(d), row_block(d), row_block(3 * d), row_block(2 * d),
            resident((d, 3 * d)), resident((d, d), MIXER),
        ],
        out_specs=[row_block(3 * d), row_block(d), pl.BlockSpec((8, 3 * d), lambda i: (0, 0))],
        out_shape=[f(3 * d, BF16), f(d, BF16), f(3 * d, F32, 8)],
        compiler_params=params(),
        cost_estimate=pl.CostEstimate(
            flops=2 * n * d * d * 8, bytes_accessed=n * d * 24, transcendentals=0
        ),
    )(dbranch, dres, packed, p, weights, mixer)


class Links:
    def __init__(self):
        self.fsdp, self.dp = lax.axis_size("fsdp"), lax.axis_size("dp")
        self.depth = self.fsdp // 2
        f, g = lax.axis_index("fsdp"), lax.axis_index("dp")
        self.place = (f * self.dp + g).astype(jnp.int32).reshape(1)
        self.coords = jnp.stack([f // 2, f % 2, g // 2, g % 2]).astype(jnp.int32)

    def square(self):
        return self.dp == 4 and self.depth == 4

    def send(self, value, core=0, a=0, b=0, z=0):
        pairs = []
        for i in range(self.fsdp * self.dp):
            f, g = divmod(i, self.dp)
            to_f = (f // 2 + z) % self.depth * 2 + (f % 2 ^ core)
            to_g = (g // 2 ^ a) * 2 + (g % 2 ^ b)
            pairs.append((i, to_f * self.dp + to_g))
        return lax.ppermute(value, AXES, pairs)


def owner(coords_ref, z, core, a, b):
    zz = lax.rem(coords_ref[0] + (4 - z), 4)
    cc = lax.rem(coords_ref[1] + core, 2)
    aa = lax.rem(coords_ref[2] + a, 2)
    bb = lax.rem(coords_ref[3] + b, 2)
    return (zz * 2 + cc) * 4 + aa * 2 + bb


def spread_small(links, block):
    own = jnp.stack([block] + [links.send(block, z=k) for k in (1, 2, 3)])
    parts = [(own, 0, 0)] + [(links.send(own, a=a, b=b), a, b) for a, b in ((0, 1), (1, 0), (1, 1))]
    pieces = []
    for value, a, b in parts:
        for core, v in ((0, value), (1, links.send(value, core=1))):
            pieces.append((v, [((k,), k, core, a, b) for k in range(4)]))
    return pieces


def spread_first(links, block):
    return [block] + [links.send(block, z=k) for k in (1, 2, 3)]


def spread_large(links, along):
    left, right = jnp.stack(along[:2]), jnp.stack(along[2:])
    left = jnp.stack([left, links.send(left, b=1)])
    right = jnp.stack([right, links.send(right, a=1)])
    parts = [
        (left, lambda i, k: (k, 0, i)), (links.send(left, a=1), lambda i, k: (k, 1, i)),
        (right, lambda i, k: (k + 2, i, 0)), (links.send(right, b=1), lambda i, k: (k + 2, i, 1)),
    ]
    pieces = []
    for value, where in parts:
        for core, v in ((0, value), (1, links.send(value, core=1))):
            places = []
            for i in range(2):
                for k in range(2):
                    z, a, b = where(i, k)
                    places.append(((i, k), z, core, a, b))
            pieces.append((v, places))
    return pieces


def assemble_kernel(coords_ref, *refs, places, rows):
    *ins, out_ref, sem = refs
    copies = []
    for value, where in zip(ins, places, strict=True):
        for index, z, core, a, b in where:
            start = pl.multiple_of(owner(coords_ref, z, core, a, b) * rows, 8)
            copies.append(
                pltpu.make_async_copy(
                    value.at[index], out_ref.at[pl.ds(start, rows)], sem.at[len(copies)]
                )
            )
            copies[-1].start()
    for copy in copies:
        copy.wait()


def assemble(links, pieces, name):
    rows, cols = pieces[0][0].shape[-2:]
    anywhere = pl.BlockSpec(memory_space=pl.ANY)
    return pl.pallas_call(
        functools.partial(assemble_kernel, places=[p[1] for p in pieces], rows=rows),
        name=name,
        in_specs=[pl.BlockSpec(memory_space=pltpu.SMEM)] + [anywhere] * len(pieces),
        out_specs=pl.BlockSpec(memory_space=pltpu.VMEM),
        out_shape=jax.ShapeDtypeStruct((32 * rows, cols), BF16),
        scratch_shapes=[pltpu.SemaphoreType.DMA((32,))],
        compiler_params=params(),
        cost_estimate=pl.CostEstimate(
            flops=0, bytes_accessed=32 * rows * cols * 4, transcendentals=0
        ),
    )(links.coords, *[p[0] for p in pieces])


def send_order():
    order = []
    for core in range(2):
        order += [(core, a, b, k) for b in range(2) for a in range(2) for k in (0, 1)]
        order += [(core, a, b, k) for a in range(2) for b in range(2) for k in (2, 3)]
    return order


def deal_kernel(coords_ref, *refs, rows, spans):
    ins, keep_ref, away_ref, sem = refs[:-3], refs[-3], refs[-2], refs[-1]
    copies = []
    for at, (core, a, b, z) in enumerate(send_order()):
        dev = owner(coords_ref, 4 - z, core, a, b)
        start = pl.multiple_of(dev * rows, 8)
        out = away_ref if core else keep_ref
        for value, (lo, hi) in zip(ins, spans, strict=True):
            copies.append(
                pltpu.make_async_copy(
                    value.at[pl.ds(start, rows)],
                    out.at[at % 16, :, lo:hi],
                    sem.at[len(copies)],
                )
            )
            copies[-1].start()
    for copy in copies:
        copy.wait()


def deal(links, grads, rows, name):
    spans, at = [], 0
    for g in grads:
        spans.append((at, at + g.shape[1]))
        at += g.shape[1]
    anywhere = pl.BlockSpec(memory_space=pl.ANY)
    vmem = pl.BlockSpec(memory_space=pltpu.VMEM)
    return pl.pallas_call(
        functools.partial(deal_kernel, rows=rows, spans=spans),
        name=name,
        in_specs=[pl.BlockSpec(memory_space=pltpu.SMEM)] + [anywhere] * len(grads),
        out_specs=[vmem, vmem],
        out_shape=[jax.ShapeDtypeStruct((16, rows, at), BF16)] * 2,
        scratch_shapes=[pltpu.SemaphoreType.DMA((32 * len(grads),))],
        compiler_params=params(),
        cost_estimate=pl.CostEstimate(
            flops=0, bytes_accessed=32 * rows * at * 4, transcendentals=0
        ),
    )(links.coords, *grads)


def add(a, b):
    return (a.astype(F32) + b.astype(F32)).astype(BF16)


def reduce_blocks(links, keep, away):
    got = links.send(away, core=1)
    part = lambda lo, hi: add(keep[lo:hi], got[lo:hi])
    left_got = links.send(part(4, 8), b=1)
    right_got = links.send(part(12, 16), a=1)
    left, right = part(0, 4), part(8, 12)
    left_got2 = links.send(add(left[2:], left_got[2:]), a=1)
    right_got2 = links.send(add(right[2:], right_got[2:]), b=1)
    left, right = add(left[:2], left_got[:2]), add(right[:2], right_got[:2])
    one = links.send(add(left[1], left_got2[1]), z=1)
    two = links.send(add(right[0], right_got2[0]), z=2)
    three = links.send(add(right[1], right_got2[1]), z=3)
    total = left[0].astype(F32) + left_got2[0].astype(F32)
    return total + one.astype(F32) + two.astype(F32) + three.astype(F32)


def gather(value):
    return lax.all_gather(value, AXES, axis=0, tiled=True)


def scatter(value):
    return lax.psum_scatter(value, AXES, scatter_dimension=0, tiled=True)


SLOTS = 24


def vector_slots(vectors):
    rows = [jnp.pad(v, (0, LANES - v.shape[0])) for v in vectors]
    rows += [jnp.zeros((LANES,), vectors[0].dtype)] * (SLOTS - len(rows))
    return jnp.stack(rows)


def unslot(slots, sizes):
    return [slots[:, k, :m].reshape(1, -1) for k, m in enumerate(sizes)]


def on_device(
    embedded, first_drop, second_drop, sent_lengths, out_cotangent,
    triple_weight, query_value_bias, mixer_weight, mixer_bias, first_gain, first_shift,
    widen_weight, widen_bias, narrow_weight, narrow_bias, second_gain, second_shift,
    pooler_weight, pooler_bias,
):
    views, sents, length, d = embedded.shape
    n = views * sents * length
    seqs = views * sents
    ff = widen_weight.shape[1]
    devices = lax.axis_size(AXES)
    links = Links()
    near = links.square() and triple_weight.shape[0] == SLOTS
    x = embedded.reshape(n, d)
    drop1 = first_drop.reshape(n, d)
    drop2 = second_drop.reshape(n, d)
    cot = out_cotangent.reshape(n, d)

    small = [
        query_value_bias, mixer_bias, first_gain, first_shift, widen_bias, narrow_bias,
        second_gain, second_shift, pooler_bias,
    ]
    sizes = [v.shape[0] for v in small]
    slots = vector_slots(small)
    narrow_rows = narrow_weight.shape[0]
    if near:
        attn_block = jnp.concatenate([triple_weight, slots], axis=1)
        ffn_block = jnp.concatenate([widen_weight, mixer_weight, pooler_weight], axis=1)
        attn_pieces = spread_small(links, attn_block)
        attn_all = assemble(links, attn_pieces, "gather_attn")
        slots_all = attn_all[:, 3 * d :].reshape(devices, SLOTS, LANES)
        ffn_all = assemble(links, spread_large(links, spread_first(links, ffn_block)), "gather_ffn")
        wn = assemble(links, spread_large(links, spread_first(links, narrow_weight)), "gather_narrow")
    else:
        attn_all = gather(triple_weight)
        slots_all = gather(slots[None])
        ffn_all = gather(jnp.concatenate([widen_weight, mixer_weight, pooler_weight], axis=1))
        wn = gather(narrow_weight)
    qv, mb, g1, s1, wwb, wnb, g2, s2, wpb = unslot(slots_all.astype(F32), sizes)
    wb = jnp.concatenate([qv[:, :d], jnp.zeros((1, d), F32), qv[:, d:]], axis=1)

    packed, p, ctx, c1, rho1, c_first, sums1 = attn_fwd(
        sent_lengths, x, drop1, attn_all, wb, ffn_all, mb, length
    )
    drop_first = second_drop[:, :, 0].reshape(seqs, d)
    unit, pooled, rho_p, first = first_tokens(
        c_first, drop_first, g1, s1, ffn_all, wwb, wn, wnb, g2, s2, wpb
    )
    if near:
        units = assemble(links, spread_small(links, unit), "gather_units").reshape(devices, seqs, d)
    else:
        units = gather(unit[None])
    one = units[:, :sents].reshape(devices * sents, d)
    two = units[:, sents:].reshape(devices * sents, d)
    hl, act, slope, c2, rho2, outputs, sums2 = ffn_fwd(
        sent_lengths, c1, drop2, g1, s1, ffn_all, wwb, wn, wnb, g2, s2, length
    )
    loss, dfirst, g_pool, g_poolb = loss_parts(links.place, one, two, pooled, rho_p, first, ffn_all)
    dnarrow, dwide, dres, dbranch, rows, wide = ffn_back(
        sent_lengths, cot, dfirst, c2, rho2, drop2, slope, c1, rho1, drop1, g1, ffn_all, wn, g2, length
    )
    g_narrow = dot_tn(act, dnarrow).astype(BF16)
    g_widen = dot_tn(hl, dwide).astype(BF16)
    g_pool = g_pool.astype(BF16)
    if near:
        s_wn = reduce_blocks(links, *deal(links, [g_narrow], narrow_rows, "deal_narrow"))
        wide_sum = reduce_blocks(links, *deal(links, [g_widen, g_pool], SLOTS, "deal_widen"))
        s_ww, s_wp = wide_sum[:, :ff], wide_sum[:, ff:]
    g_mixer = dot_tn(ctx, dbranch).astype(BF16)
    dpacked, dx, packed_sums = attn_back(dbranch, dres, packed, p, attn_all, ffn_all)
    g_triple = dot_tn(x, dpacked).astype(BF16)

    count = 2.0 * jnp.sum(sent_lengths).astype(F32)
    sq = [jnp.sum(sums1[:, 0]), jnp.sum(sums1[:, 1]), jnp.sum(sums2), count]
    qvg = jnp.concatenate([packed_sums[0, :d], packed_sums[0, 2 * d :]])
    vec = [qvg, rows[5], rows[3], rows[4], wide[0], rows[2], rows[0], rows[1], g_poolb[0]]
    vec = [jnp.pad(v.reshape(devices, -1), ((0, 0), (0, LANES - m))) for v, m in zip(vec, sizes)]
    vec += [jnp.broadcast_to(v, (devices, LANES)) for v in sq]
    vec += [jnp.zeros((devices, LANES), F32)] * (SLOTS - len(vec))
    vec = jnp.stack(vec, axis=1)
    if near:
        vec = vec.reshape(devices * SLOTS, LANES).astype(BF16)
        attn_sum = reduce_blocks(links, *deal(links, [g_triple, g_mixer, vec], SLOTS, "deal_attn"))
        s_w, s_m, got = attn_sum[:, : 3 * d], attn_sum[:, 3 * d : 4 * d], attn_sum[:, 4 * d :]
    else:
        s_w, s_m, s_ww, s_wn, s_wp = (
            scatter(g).astype(F32) for g in (g_triple, g_mixer, g_widen, g_narrow, g_pool)
        )
        got = scatter(vec)[0]
    sums = got[len(small) : len(small) + 4, 0]
    rms = jnp.sqrt(sums[:3] / (sums[3] * d))
    got = [got[k, :m] for k, m in enumerate(sizes)]
    return (
        loss[0, 0], outputs.reshape(embedded.shape), dx.reshape(embedded.shape), rms,
        s_w, got[0], s_m, got[1], got[2], got[3], s_ww, got[4], s_wn, got[5], got[6], got[7],
        s_wp, got[8],
    )


def solution(mesh):
    rows4 = P(None, AXES, None, None)
    mat, vec = P(AXES, None), P(AXES)
    in_specs = (
        rows4, rows4, rows4, vec, rows4,
        mat, vec, mat, vec, vec, vec, mat, vec, mat, vec, vec, vec, mat, vec,
    )
    out_specs = (
        P(), rows4, rows4, P(), mat, vec, mat, vec, vec, vec, mat, vec, mat, vec, vec, vec, mat, vec,
    )
    return jax.shard_map(
        on_device, mesh=mesh, in_specs=in_specs, out_specs=out_specs, check_vma=False
    )
```
